32 devices in a mesh: frame: 8 (over z, y), space: 4 (over x, core).
Axes of the slice: x: 2, y: 2, z: 4, core: 2. Of those that a mesh axis runs over, the one named last changes fastest.
Arguments:
- queries: float32 [8, 1024, 1120], P('frame', 'space'), may hold values from -6 to 6
- keys: float32 [8, 1024, 1120], P('frame', 'space'), may hold values from -6 to 6
- values: float32 [8, 1024, 1120], P('frame', 'space'), may hold values from -6 to 6
- cotangent: float32 [8, 1024, 1120], P('frame', 'space'), may hold values from -6 to 6
Outputs:
- query_grad: float32 [8, 1024, 1120], P('frame', 'space')
- key_grad: float32 [8, 1024, 1120], P('frame', 'space')
- value_grad: float32 [8, 1024, 1120], P('frame', 'space')
The draws below stay inside these ranges and needn't reach their ends.
All inputs are finite; a program needn't handle non-finite values.
Results may differ from the reference program's by a relative error of at most 0.0003.
Values sent between devices are 32-bit elements; how exact they have to be, the bound alone decides.
A program may use at most 64 MiB of HBM per device.

```python
import jax
import jax.numpy as jnp
from jax import lax

HEAD = 112
D = 1120
FRAMES = 8
SPATIAL = 1024


def draw_field(key, salt):
    base = jax.random.fold_in(key, salt)
    entry_key = jax.random.fold_in(base, 0)
    field = jax.random.normal(entry_key, (FRAMES, SPATIAL, D), jnp.float32)
    return jnp.clip(field, -6.0, 6.0)


def draw_queries(key, part):
    return draw_field(key, 101)


def draw_keys(key, part):
    return draw_field(key, 202)


def draw_values(key, part):
    return draw_field(key, 303)


def draw_cotangent(key, part):
    return draw_field(key, 404)


def setup_inputs(seed: int = 0) -> dict:
    seeds = jax.random.split(jax.random.key(seed), 5)
    queries = draw_queries(jax.random.fold_in(seeds[4], 71), 0)
    keys = draw_keys(jax.random.fold_in(seeds[4], 71), 0)
    values = draw_values(jax.random.fold_in(seeds[4], 71), 0)
    cotangent = draw_cotangent(jax.random.fold_in(seeds[4], 71), 0)
    return {"queries": queries, "keys": keys, "values": values, "cotangent": cotangent}


def outer_states(left, right):
    frames, spatial, model_width = left.shape
    head_count = model_width // HEAD
    left_heads = left.reshape(frames, spatial, head_count, HEAD)
    right_heads = right.reshape(frames, spatial, head_count, HEAD)
    result = jnp.einsum('fshi,fshj->fihj', left_heads, right_heads, precision=lax.Precision.HIGHEST)
    return result.reshape(frames, HEAD, model_width)

def reference(queries, keys, values, cotangent):
    frames, spatial, model_width = queries.shape
    head_count = model_width // HEAD
    counts = (jnp.arange(frames, dtype=jnp.int32) + 1).astype(jnp.float32) * (spatial * HEAD)
    scales = 1.0 / jnp.sqrt(counts)
    pos_q = jnp.maximum(queries, 0.0)
    pos_k = jnp.maximum(keys, 0.0)
    kv_block = outer_states(pos_k, values)
    qd_block = outer_states(pos_q, cotangent) * scales[:, None, None]
    state = jnp.cumsum(kv_block, axis=0).reshape(frames, HEAD, head_count, HEAD)
    grad_state = jnp.flip(jnp.cumsum(jnp.flip(qd_block, 0), axis=0), 0).reshape(frames, HEAD, head_count, HEAD)
    cot_heads = cotangent.reshape(frames, spatial, head_count, HEAD)
    val_heads = values.reshape(frames, spatial, head_count, HEAD)
    posk_heads = pos_k.reshape(frames, spatial, head_count, HEAD)
    hp = lax.Precision.HIGHEST
    query_grad = jnp.einsum('fshj,fihj->fshi', cot_heads, state, precision=hp).reshape(frames, spatial, model_width)
    query_grad = jnp.where(queries > 0, query_grad * scales[:, None, None], 0.0)
    key_grad = jnp.einsum('fshj,fihj->fshi', val_heads, grad_state, precision=hp).reshape(frames, spatial, model_width)
    key_grad = jnp.where(keys > 0, key_grad, 0.0)
    value_grad = jnp.einsum('fshi,fihj->fshj', posk_heads, grad_state, precision=hp).reshape(frames, spatial, model_width)
    return (query_grad, key_grad, value_grad)
```

```python
import functools

import jax
import jax.numpy as jnp
from jax import lax
from jax.experimental import pallas as pl
from jax.experimental.pallas import tpu as pltpu
from jax.sharding import PartitionSpec as P

HEAD = 112
LANE = 128
GROUP = 256
CORES = 2
PAIR = 2
MESH = pl.DeviceIdType.MESH
NT = (((1,), (1,)), ((), ()))
NN = (((1,), (0,)), ((), ()))


def groups(width):
    found = []
    for start in range(0, width, GROUP):
        stop = min(start + GROUP, width)
        first, last = start // HEAD, (stop - 1) // HEAD
        left = first * HEAD // LANE * LANE
        right = min(-(-(last + 1) * HEAD // LANE) * LANE, width)
        found.append((start, stop, first, last, left, right))
    return found


def split(x):
    high = x.astype(jnp.bfloat16)
    return high, (x - high.astype(jnp.float32)).astype(jnp.bfloat16)


def dot3(a, b, dims):
    (ah, al), (bh, bl) = a, b
    dot = functools.partial(
        lax.dot_general, dimension_numbers=dims, preferred_element_type=jnp.float32
    )
    return dot(ah, bh) + dot(al, bh) + dot(ah, bl)


def outer(left_ref, right_ref, out_ref, factor):
    rows, width = left_ref.shape
    for start, stop, first, last, left, right in groups(width):
        lhs = jnp.maximum(left_ref[:, left:right], 0.0).T
        lhs = lhs[first * HEAD - left : (last + 1) * HEAD - left]
        product = dot3(split(lhs), split(right_ref[:, start:stop]), NN)
        for at in range(start, stop, LANE):
            size = min(LANE, stop - at)
            columns = product[:, at - start : at - start + size]
            lane = lax.broadcasted_iota(jnp.int32, (HEAD, size), 1) + at
            total = None
            for head in range(at // HEAD, (at + size - 1) // HEAD + 1):
                block = columns[(head - first) * HEAD : (head - first + 1) * HEAD]
                total = block if total is None else jnp.where(lane >= head * HEAD, block, total)
            total = total * factor
            if size < LANE:
                total = jnp.concatenate(
                    [total, jnp.zeros((HEAD, LANE - size), jnp.float32)], axis=1
                )
            out_ref[at // LANE, 0:HEAD, :] = total


def exchange(
    frames, chips, spatial_total, inner_rows,
    q_hbm, k_hbm, v_hbm, c_hbm, out_hbm,
    first_l, first_r, second_l, second_r,
    part_a, part_b, recv_a, chip, recv_b, own, recv_c, recv_e, send_e, state,
    load_sem, a_sem, b_send, b_recv, c_sem, e_sem, x_send, x_recv, m_sem, f_send, f_recv, out_sem,
):
    f, s = lax.axis_index("frame"), lax.axis_index("space")
    x, c = s // CORES, s % CORES
    tiles = part_a.shape[0]
    piece = own.shape[1]
    twin = (f, s + 1 - CORES * c)
    mate = (f + 1 - PAIR * (f % PAIR), s)
    step = jnp.where(c == 0, PAIR, -PAIR)
    order = jnp.where(c == 0, f, frames - 1 - f)
    u, odd = order // PAIR, order % PAIR
    last_u = frames // PAIR - 1
    has_before, has_after = u > 0, u < last_u
    before = (jnp.where(has_before, f - step, f), s)
    after = (jnp.where(has_after, f + step, f), s)

    def chip_at(d):
        return (f, (x + d) % chips * CORES + c)

    def remote(src, dst, sems, recv, device):
        return pltpu.make_async_remote_copy(
            src_ref=src, dst_ref=dst, send_sem=sems, recv_sem=recv,
            device_id=device, device_id_type=MESH,
        )

    barrier = pltpu.get_barrier_semaphore()
    partners = [twin, mate] + [chip_at(d) for d in range(1, chips)]
    for device in partners:
        pl.semaphore_signal(barrier, inc=1, device_id=device, device_id_type=MESH)

    @pl.when(has_before)
    def _():
        pl.semaphore_signal(barrier, inc=1, device_id=before, device_id_type=MESH)

    @pl.when(has_after)
    def _():
        pl.semaphore_signal(barrier, inc=1, device_id=after, device_id_type=MESH)

    slots = (first_l, first_r, second_l, second_r)
    for core, sources in enumerate(((q_hbm, c_hbm, k_hbm, v_hbm), (k_hbm, v_hbm, q_hbm, c_hbm))):

        @pl.when(c == core)
        def _():
            for at in range(4):
                pltpu.make_async_copy(sources[at].at[0], slots[at], load_sem.at[at]).start()

    counts = jnp.full((1, LANE), (f + 1) * (spatial_total * HEAD), jnp.int32)
    scale = (1.0 / jnp.sqrt(counts.astype(jnp.float32)))[0:1, 0:1]

    for at in range(2):
        pltpu.make_async_copy(q_hbm.at[0], slots[at], load_sem.at[at]).wait()
    if inner_rows > HEAD:
        part_a[:, HEAD:, :] = jnp.zeros((tiles, inner_rows - HEAD, LANE), jnp.float32)
        part_b[:, HEAD:, :] = jnp.zeros((tiles, inner_rows - HEAD, LANE), jnp.float32)
    outer(first_l, first_r, part_a, jnp.where(c == 0, scale, 1.0))

    pl.semaphore_wait(
        barrier, len(partners) + has_before.astype(jnp.int32) + has_after.astype(jnp.int32)
    )

    def copy_a(t):
        return remote(part_a.at[t], recv_a.at[t], a_sem.at[0, t], a_sem.at[1, t], twin)

    def copy_b(d, t):
        rows = pl.ds(pl.multiple_of((x + d) % chips * piece, 8), piece)
        return remote(
            chip.at[t, rows], recv_b.at[d - 1, t],
            b_send.at[d - 1, t], b_recv.at[d - 1, t], chip_at(d),
        )

    def copy_c(t):
        return remote(own.at[t], recv_c.at[t], c_sem.at[0, t], c_sem.at[1, t], mate)

    def copy_e(t):
        return remote(send_e.at[t], recv_e.at[t], e_sem.at[0, t], e_sem.at[1, t], after)

    mine = pl.ds(pl.multiple_of(x * piece, 8), piece)

    def rows_at(d):
        return pl.ds(pl.multiple_of((x + chips - d) % chips * piece, 8), piece)

    def copy_x(d, t):
        here = state.at[c, t, mine]
        return remote(here, here, x_send.at[d - 1, t], x_recv.at[d - 1, t], chip_at(d))

    def copy_m(t):
        here = state.at[c, t, mine]
        return remote(here, here, m_sem.at[0, t], m_sem.at[1, t], twin)

    def copy_f(d, t):
        here = state.at[c, t, rows_at(d)]
        return remote(here, here, f_send.at[d - 1, t], f_recv.at[d - 1, t], twin)

    for t in range(tiles):
        copy_a(t).start()
    for at in range(2, 4):
        pltpu.make_async_copy(q_hbm.at[0], slots[at], load_sem.at[at]).wait()
    outer(second_l, second_r, part_b, jnp.where(c == 1, scale, 1.0))

    def phase_b(t):
        copy_a(t).wait_recv()
        chip[t] = part_b[t] + recv_a[t]
        for d in range(1, chips):
            copy_b(d, t).start()

    def phase_c(t):
        total = chip[t, mine]
        for d in range(1, chips):
            copy_b(d, t).wait_recv()
            total = total + recv_b[d - 1, t]
        own[t] = total
        copy_c(t).start()

    def share(t, entering):
        keep = jnp.where(odd == 1, recv_c[t], 0.0) + own[t]
        state[c, t, mine] = keep if entering is None else keep + entering
        for d in range(1, chips):
            copy_x(d, t).start()
        copy_m(t).start()

    def phase_d(t):
        copy_c(t).wait_recv()

        @pl.when(jnp.logical_not(has_before))
        def _():
            if last_u > 0:
                send_e[t] = own[t] + recv_c[t]
                copy_e(t).start()
            share(t, None)

    def phase_e(t, rank, last):
        @pl.when(u >= rank if last else u == rank)
        def _():
            copy_e(t).wait_recv()

            @pl.when(has_after)
            def _():
                send_e[t] = recv_e[t] + own[t] + recv_c[t]
                copy_e(t).start()

            share(t, recv_e[t])

    def phase_f(t):
        for d in range(1, chips):
            copy_x(d, t).wait_recv()
            copy_f(d, t).start()

    events = []
    for t in range(tiles):
        events.append((0.1 * t, 0, functools.partial(phase_b, t)))
        events.append((2.0 + 0.62 * t, 1, functools.partial(phase_c, t)))
        events.append((4.2 + 0.62 * t, 2, functools.partial(phase_d, t)))
        ranks = min(last_u, 3)
        for rank in range(1, ranks + 1):
            events.append((
                4.2 + 2.0 * rank + 0.62 * t, 2 + rank,
                functools.partial(phase_e, t, rank, rank == ranks),
            ))
        events.append((13.0 + 0.62 * t, 9, functools.partial(phase_f, t)))
    for _, _, run in sorted(events, key=lambda e: e[:2]):
        run()

    done = pltpu.make_async_copy(state.at[c], out_hbm.at[c], out_sem.at[0])
    done.start()
    for t in range(tiles):
        copy_m(t).wait_recv()
        for d in range(1, chips):
            copy_f(d, t).wait_recv()
    twin_done = pltpu.make_async_copy(state.at[1 - c], out_hbm.at[1 - c], out_sem.at[1])
    twin_done.start()
    for t in range(tiles):
        copy_a(t).wait_send()
        copy_c(t).wait_send()
        copy_m(t).wait_send()
        for d in range(1, chips):
            copy_b(d, t).wait_send()
            copy_x(d, t).wait_send()
            copy_f(d, t).wait_send()

    if last_u > 0:

        @pl.when(has_after)
        def _():
            for t in range(tiles):
                copy_e(t).wait_send()

    done.wait()
    twin_done.wait()


def spread(state, start, stop, left, right):
    columns = jnp.concatenate(
        [state[t] for t in range(left // LANE, -(-right // LANE))], axis=1
    )[:, : right - left]
    blocks = []
    for head in range(start // HEAD, (stop - 1) // HEAD + 1):
        top, end = max(start - head * HEAD, 0), min(stop - head * HEAD, HEAD)
        block = columns[top:end]
        lane = lax.broadcasted_iota(jnp.int32, block.shape, 1) + left
        blocks.append(
            jnp.where((lane >= head * HEAD) & (lane < (head + 1) * HEAD), block, 0.0)
        )
    return jnp.concatenate(blocks, axis=0)


def apply(spatial_total, s_ref, q_ref, k_ref, v_ref, c_ref, qg_ref, kg_ref, vg_ref, kv_nt, qd_nt, qd_nn):
    width = q_ref.shape[-1]
    parts = groups(width)
    f = lax.axis_index("frame")

    @pl.when(pl.program_id(0) == 0)
    def _():
        counts = jnp.full((1, LANE), (f + 1) * (spatial_total * HEAD), jnp.int32)
        scale = (1.0 / jnp.sqrt(counts.astype(jnp.float32)))[None, :, :]
        states = (s_ref[0][:, 0:HEAD] * scale, s_ref[1][:, 0:HEAD])
        for g, (start, stop, _, _, left, right) in enumerate(parts):
            for ref, state in zip((kv_nt, qd_nt), states):
                high, low = split(spread(state, start, stop, left, right))
                ref[0, g, 0 : stop - start, 0 : right - left] = high
                ref[1, g, 0 : stop - start, 0 : right - left] = low
            high, low = split(spread(states[1], left, right, start, stop))
            qd_nn[0, g, 0 : right - left, 0 : stop - start] = high
            qd_nn[1, g, 0 : right - left, 0 : stop - start] = low

    for g, (start, stop, _, _, left, right) in enumerate(parts):
        here = slice(0, stop - start), slice(0, right - left)

        def weights(ref, at):
            return ref[(0, g) + at], ref[(1, g) + at]

        cot = split(c_ref[0, :, left:right])
        qg = dot3(cot, weights(kv_nt, here), NT)
        qg_ref[0, :, start:stop] = jnp.where(q_ref[0, :, start:stop] > 0, qg, 0.0)
        val = split(v_ref[0, :, left:right])
        kg = dot3(val, weights(qd_nt, here), NT)
        kg_ref[0, :, start:stop] = jnp.where(k_ref[0, :, start:stop] > 0, kg, 0.0)
        pos = split(jnp.maximum(k_ref[0, :, left:right], 0.0))
        vg_ref[0, :, start:stop] = dot3(pos, weights(qd_nn, here[::-1]), NN)


def shards(frames, chips, queries, keys, values, cotangent):
    _, spatial, width = queries.shape
    spatial_total = spatial * chips * CORES
    tiles = -(-width // LANE)
    piece = -(-HEAD // (8 * chips)) * 8
    rows = piece * chips
    full = pltpu.VMEM((tiles, rows, LANE), jnp.float32)
    part = pltpu.VMEM((tiles, piece, LANE), jnp.float32)
    load = pltpu.VMEM((spatial, width), jnp.float32)
    dma = pltpu.SemaphoreType.DMA
    others = max(chips - 1, 1)
    anywhere = pl.BlockSpec(memory_space=pl.ANY)
    state = pl.pallas_call(
        functools.partial(exchange, frames, chips, spatial_total, rows),
        out_shape=jax.ShapeDtypeStruct((2, tiles, rows, LANE), jnp.float32),
        in_specs=[anywhere] * 4,
        out_specs=anywhere,
        scratch_shapes=[load] * 4
        + [full, full, full, full, pltpu.VMEM((others, tiles, piece, LANE), jnp.float32)]
        + [part, part, part, part, pltpu.VMEM((2, tiles, rows, LANE), jnp.float32)]
        + [dma((4,)), dma((2, tiles)), dma((others, tiles)), dma((others, tiles))]
        + [dma((2, tiles)), dma((2, tiles)), dma((others, tiles)), dma((others, tiles))]
        + [dma((2, tiles)), dma((others, tiles)), dma((others, tiles)), dma((2,))],
        compiler_params=pltpu.CompilerParams(collective_id=0, has_side_effects=True),
        name="exchange",
    )(queries, keys, values, cotangent)
    block = min(spatial, LANE)
    slab = pl.BlockSpec((1, block, width), lambda r: (0, r, 0))
    parts = groups(width)
    window = max(right - left for *_, left, right in parts)
    shape = jax.ShapeDtypeStruct(queries.shape, jnp.float32)
    return pl.pallas_call(
        functools.partial(apply, spatial_total),
        grid=(spatial // block,),
        out_shape=(shape,) * 3,
        in_specs=[pl.BlockSpec((2, tiles, rows, LANE), lambda r: (0, 0, 0, 0))] + [slab] * 4,
        out_specs=(slab,) * 3,
        scratch_shapes=[
            pltpu.VMEM((2, len(parts), GROUP, window), jnp.bfloat16),
            pltpu.VMEM((2, len(parts), GROUP, window), jnp.bfloat16),
            pltpu.VMEM((2, len(parts), window, GROUP), jnp.bfloat16),
        ],
        name="apply",
    )(state, queries, keys, values, cotangent)


def solution(mesh):
    placed = P("frame", "space", None)
    frames, space = mesh.shape["frame"], mesh.shape["space"]
    return jax.shard_map(
        functools.partial(shards, frames, space // CORES),
        mesh=mesh,
        in_specs=(placed,) * 4,
        out_specs=(placed,) * 3,
        check_vma=False,
    )
```

```python
import functools

import jax
import jax.numpy as jnp
from jax import lax
from jax.experimental import pallas as pl
from jax.experimental.pallas import tpu as pltpu
from jax.sharding import PartitionSpec as P

HEAD = 112
LANE = 128
GROUP = 256
CORES = 2
PAIR = 2
MESH = pl.DeviceIdType.MESH
NT = (((1,), (1,)), ((), ()))
NN = (((1,), (0,)), ((), ()))


def groups(width):
    found = []
    for start in range(0, width, GROUP):
        stop = min(start + GROUP, width)
        found.append((start, stop, start // HEAD, (stop - 1) // HEAD))
    return found


def split(x):
    high = x.astype(jnp.bfloat16)
    return high, (x - high.astype(jnp.float32)).astype(jnp.bfloat16)


def dot3(a, b, dims):
    (ah, al), (bh, bl) = a, b
    dot = functools.partial(
        lax.dot_general, dimension_numbers=dims, preferred_element_type=jnp.float32
    )
    return dot(ah, bh) + dot(al, bh) + dot(ah, bl)


def outer(left_ref, right_ref, out_ref, factor, ready):
    for start, stop, first, last in groups(left_ref.shape[0]):
        lhs = jnp.maximum(left_ref[first * HEAD : (last + 1) * HEAD], 0.0)
        product = dot3(split(lhs), split(right_ref[start:stop]), NT)
        for at in range(start, stop, LANE):
            size = min(LANE, stop - at)
            columns = product[:, at - start : at - start + size]
            lane = lax.broadcasted_iota(jnp.int32, (HEAD, size), 1) + at
            total = None
            for head in range(at // HEAD, (at + size - 1) // HEAD + 1):
                block = columns[(head - first) * HEAD : (head - first + 1) * HEAD]
                total = block if total is None else jnp.where(lane >= head * HEAD, block, total)
            total = total * factor
            if size < LANE:
                total = jnp.concatenate(
                    [total, jnp.zeros((HEAD, LANE - size), jnp.float32)], axis=1
                )
            out_ref[at // LANE, 0:HEAD, :] = total
            ready(at // LANE)


def exchange(
    frames, chips, spatial_total, inner_rows,
    q_hbm, k_hbm, v_hbm, c_hbm, out_hbm,
    first_l, first_r, second_l, second_r,
    part_a, part_b, recv_a, chip, recv_b, own, recv_c, recv_e, send_e, state,
    load_sem, a_sem, b_send, b_recv, c_sem, e_sem, x_send, x_recv, m_sem, f_send, f_recv, out_sem,
):
    f, s = lax.axis_index("frame"), lax.axis_index("space")
    x, c = s // CORES, s % CORES
    tiles = part_a.shape[0]
    piece = own.shape[1]
    twin = (f, s + 1 - CORES * c)
    mate = (f + 1 - PAIR * (f % PAIR), s)
    step = jnp.where(c == 0, PAIR, -PAIR)
    order = jnp.where(c == 0, f, frames - 1 - f)
    u, odd = order // PAIR, order % PAIR
    last_u = frames // PAIR - 1
    has_before, has_after = u > 0, u < last_u
    before = (jnp.where(has_before, f - step, f), s)
    after = (jnp.where(has_after, f + step, f), s)

    def chip_at(d):
        return (f, (x + d) % chips * CORES + c)

    def remote(src, dst, sems, recv, device):
        return pltpu.make_async_remote_copy(
            src_ref=src, dst_ref=dst, send_sem=sems, recv_sem=recv,
            device_id=device, device_id_type=MESH,
        )

    barrier = pltpu.get_barrier_semaphore()
    partners = [twin, mate] + [chip_at(d) for d in range(1, chips)]
    for device in partners:
        pl.semaphore_signal(barrier, inc=1, device_id=device, device_id_type=MESH)

    @pl.when(has_before)
    def _():
        pl.semaphore_signal(barrier, inc=1, device_id=before, device_id_type=MESH)

    @pl.when(has_after)
    def _():
        pl.semaphore_signal(barrier, inc=1, device_id=after, device_id_type=MESH)

    slots = (first_l, first_r, second_l, second_r)
    for core, sources in enumerate(((q_hbm, c_hbm, k_hbm, v_hbm), (k_hbm, v_hbm, q_hbm, c_hbm))):

        @pl.when(c == core)
        def _():
            for at in range(4):
                pltpu.make_async_copy(sources[at].at[0], slots[at], load_sem.at[at]).start()

    counts = jnp.full((1, LANE), (f + 1) * (spatial_total * HEAD), jnp.int32)
    scale = (1.0 / jnp.sqrt(counts.astype(jnp.float32)))[0:1, 0:1]

    for at in range(2):
        pltpu.make_async_copy(q_hbm.at[0], slots[at], load_sem.at[at]).wait()
    if inner_rows > HEAD:
        part_a[:, HEAD:, :] = jnp.zeros((tiles, inner_rows - HEAD, LANE), jnp.float32)
        part_b[:, HEAD:, :] = jnp.zeros((tiles, inner_rows - HEAD, LANE), jnp.float32)
    def copy_a(t):
        return remote(part_a.at[t], recv_a.at[t], a_sem.at[0, t], a_sem.at[1, t], twin)

    def copy_b(d, t):
        rows = pl.ds(pl.multiple_of((x + d) % chips * piece, 8), piece)
        return remote(
            chip.at[t, rows], recv_b.at[d - 1, t],
            b_send.at[d - 1, t], b_recv.at[d - 1, t], chip_at(d),
        )

    def copy_c(t):
        return remote(own.at[t], recv_c.at[t], c_sem.at[0, t], c_sem.at[1, t], mate)

    def copy_e(t):
        return remote(send_e.at[t], recv_e.at[t], e_sem.at[0, t], e_sem.at[1, t], after)

    mine = pl.ds(pl.multiple_of(x * piece, 8), piece)

    def rows_at(d):
        return pl.ds(pl.multiple_of((x + chips - d) % chips * piece, 8), piece)

    def copy_x(d, t):
        here = state.at[c, t, mine]
        return remote(here, here, x_send.at[d - 1, t], x_recv.at[d - 1, t], chip_at(d))

    def copy_m(t):
        here = state.at[c, t, mine]
        return remote(here, here, m_sem.at[0, t], m_sem.at[1, t], twin)

    def copy_f(d, t):
        here = state.at[c, t, rows_at(d)]
        return remote(here, here, f_send.at[d - 1, t], f_recv.at[d - 1, t], twin)

    def send_first(t):
        if t == 0:
            pl.semaphore_wait(
                barrier, len(partners) + has_before.astype(jnp.int32) + has_after.astype(jnp.int32)
            )
        copy_a(t).start()

    outer(first_l, first_r, part_a, jnp.where(c == 0, scale, 1.0), send_first)
    for at in range(2, 4):
        pltpu.make_async_copy(q_hbm.at[0], slots[at], load_sem.at[at]).wait()
    outer(second_l, second_r, part_b, jnp.where(c == 1, scale, 1.0), lambda t: None)

    def phase_b(t):
        copy_a(t).wait_recv()
        chip[t] = part_b[t] + recv_a[t]
        for d in range(1, chips):
            copy_b(d, t).start()

    def phase_c(t):
        total = chip[t, mine]
        for d in range(1, chips):
            copy_b(d, t).wait_recv()
            total = total + recv_b[d - 1, t]
        own[t] = total
        copy_c(t).start()

    def share(t, entering):
        keep = jnp.where(odd == 1, recv_c[t], 0.0) + own[t]
        state[c, t, mine] = keep if entering is None else keep + entering
        for d in range(1, chips):
            copy_x(d, t).start()
        copy_m(t).start()

    def phase_d(t):
        copy_c(t).wait_recv()

        @pl.when(jnp.logical_not(has_before))
        def _():
            if last_u > 0:
                send_e[t] = own[t] + recv_c[t]
                copy_e(t).start()
            share(t, None)

    def phase_e(t, rank, last):
        @pl.when(u >= rank if last else u == rank)
        def _():
            copy_e(t).wait_recv()

            @pl.when(has_after)
            def _():
                send_e[t] = recv_e[t] + own[t] + recv_c[t]
                copy_e(t).start()

            share(t, recv_e[t])

    def phase_f(t):
        for d in range(1, chips):
            copy_x(d, t).wait_recv()
            copy_f(d, t).start()

    events = []
    for t in range(tiles):
        events.append((0.1 * t, 0, functools.partial(phase_b, t)))
        events.append((2.0 + 0.62 * t, 1, functools.partial(phase_c, t)))
        events.append((4.2 + 0.62 * t, 2, functools.partial(phase_d, t)))
        ranks = min(last_u, 3)
        for rank in range(1, ranks + 1):
            events.append((
                4.2 + 2.0 * rank + 0.62 * t, 2 + rank,
                functools.partial(phase_e, t, rank, rank == ranks),
            ))
        events.append((13.0 + 0.62 * t, 9, functools.partial(phase_f, t)))
    for _, _, run in sorted(events, key=lambda e: e[:2]):
        run()

    done = pltpu.make_async_copy(state.at[c], out_hbm.at[c], out_sem.at[0])
    done.start()
    for t in range(tiles):
        copy_m(t).wait_recv()
        for d in range(1, chips):
            copy_f(d, t).wait_recv()
    twin_done = pltpu.make_async_copy(state.at[1 - c], out_hbm.at[1 - c], out_sem.at[1])
    twin_done.start()
    for t in range(tiles):
        copy_a(t).wait_send()
        copy_c(t).wait_send()
        copy_m(t).wait_send()
        for d in range(1, chips):
            copy_b(d, t).wait_send()
            copy_x(d, t).wait_send()
            copy_f(d, t).wait_send()

    if last_u > 0:

        @pl.when(has_after)
        def _():
            for t in range(tiles):
                copy_e(t).wait_send()

    done.wait()
    twin_done.wait()


def stacked(state):
    high, low = split(state)
    return jnp.concatenate([high, low], axis=0)


def product(weights, x):
    high, low = split(x)
    dot = functools.partial(
        lax.dot_general, dimension_numbers=NN, preferred_element_type=jnp.float32
    )
    both = dot(weights, high)
    return both[:HEAD] + both[HEAD:] + dot(weights[:HEAD], low)


def apply(spatial_total, s_ref, q_ref, k_ref, v_ref, c_ref, qg_ref, kg_ref, vg_ref, kv, qd, qd_t):
    heads = kv.shape[0]
    f = lax.axis_index("frame")

    @pl.when(pl.program_id(0) == 0)
    def _():
        counts = jnp.full((1, LANE), (f + 1) * (spatial_total * HEAD), jnp.int32)
        scale = (1.0 / jnp.sqrt(counts.astype(jnp.float32)))[:, :HEAD]
        for head in range(heads):
            low = head * HEAD // LANE
            high = ((head + 1) * HEAD - 1) // LANE
            offset = head * HEAD - low * LANE

            def pick(at):
                wide = jnp.concatenate(
                    [s_ref[at, t, 0:HEAD, :] for t in range(low, high + 1)], axis=1
                )
                return wide[:, offset : offset + HEAD]

            kv[head] = stacked(pick(0) * scale)
            grad = pick(1)
            qd[head] = stacked(grad)
            qd_t[head] = stacked(grad.T)

    count = q_ref.shape[1] // HEAD
    for at in range(count):
        head = pl.program_id(0) * count + at
        rows = slice(at * HEAD, (at + 1) * HEAD)
        keys = k_ref[0, rows]
        qg_ref[0, rows] = jnp.where(q_ref[0, rows] > 0, product(kv[head], c_ref[0, rows]), 0.0)
        kg_ref[0, rows] = jnp.where(keys > 0, product(qd[head], v_ref[0, rows]), 0.0)
        vg_ref[0, rows] = product(qd_t[head], jnp.maximum(keys, 0.0))


def shards(frames, chips, queries, keys, values, cotangent):
    queries, keys, values, cotangent = (
        jnp.swapaxes(a, 1, 2) for a in (queries, keys, values, cotangent)
    )
    _, width, spatial = queries.shape
    spatial_total = spatial * chips * CORES
    tiles = -(-width // LANE)
    piece = -(-HEAD // (8 * chips)) * 8
    rows = piece * chips
    full = pltpu.VMEM((tiles, rows, LANE), jnp.float32)
    part = pltpu.VMEM((tiles, piece, LANE), jnp.float32)
    load = pltpu.VMEM((width, spatial), jnp.float32)
    dma = pltpu.SemaphoreType.DMA
    others = max(chips - 1, 1)
    anywhere = pl.BlockSpec(memory_space=pl.ANY)
    state = pl.pallas_call(
        functools.partial(exchange, frames, chips, spatial_total, rows),
        out_shape=jax.ShapeDtypeStruct((2, tiles, rows, LANE), jnp.float32),
        in_specs=[anywhere] * 4,
        out_specs=anywhere,
        scratch_shapes=[load] * 4
        + [full, full, full, full, pltpu.VMEM((others, tiles, piece, LANE), jnp.float32)]
        + [part, part, part, part, pltpu.VMEM((2, tiles, rows, LANE), jnp.float32)]
        + [dma((4,)), dma((2, tiles)), dma((others, tiles)), dma((others, tiles))]
        + [dma((2, tiles)), dma((2, tiles)), dma((others, tiles)), dma((others, tiles))]
        + [dma((2, tiles)), dma((others, tiles)), dma((others, tiles)), dma((2,))],
        compiler_params=pltpu.CompilerParams(collective_id=0, has_side_effects=True),
        name="exchange",
    )(queries, keys, values, cotangent)
    heads = width // HEAD
    steps = heads // 2 if heads % 2 == 0 else heads
    slab = pl.BlockSpec((1, width // steps, spatial), lambda r: (0, r, 0))
    shape = jax.ShapeDtypeStruct(queries.shape, jnp.float32)
    weights = pltpu.VMEM((heads, 2 * HEAD, HEAD), jnp.bfloat16)
    grads = pl.pallas_call(
        functools.partial(apply, spatial_total),
        grid=(steps,),
        out_shape=(shape,) * 3,
        in_specs=[pl.BlockSpec((2, tiles, rows, LANE), lambda r: (0, 0, 0, 0))] + [slab] * 4,
        out_specs=(slab,) * 3,
        scratch_shapes=[weights] * 3,
        name="apply",
    )(state, queries, keys, values, cotangent)
    return tuple(jnp.swapaxes(a, 1, 2) for a in grads)


def solution(mesh):
    placed = P("frame", "space", None)
    frames, space = mesh.shape["frame"], mesh.shape["space"]
    return jax.shard_map(
        functools.partial(shards, frames, space // CORES),
        mesh=mesh,
        in_specs=(placed,) * 4,
        out_specs=(placed,) * 3,
        check_vma=False,
    )
```

```python
import functools

import jax
import jax.numpy as jnp
from jax import lax
from jax.experimental import pallas as pl
from jax.experimental.pallas import tpu as pltpu
from jax.sharding import PartitionSpec as P

HEAD = 112
LANE = 128
GROUP = 256
CORES = 2
PAIR = 2
VMEM_LIMIT = 32 * 2**20
MESH = pl.DeviceIdType.MESH
NT = (((1,), (1,)), ((), ()))
NN = (((1,), (0,)), ((), ()))


def groups(width):
    found = []
    for start in range(0, width, GROUP):
        stop = min(start + GROUP, width)
        found.append((start, stop, start // HEAD, (stop - 1) // HEAD))
    return found


def split(x):
    high = x.astype(jnp.bfloat16)
    return high, (x - high.astype(jnp.float32)).astype(jnp.bfloat16)


def dot3(a, b, dims):
    (ah, al), (bh, bl) = a, b
    dot = functools.partial(
        lax.dot_general, dimension_numbers=dims, preferred_element_type=jnp.float32
    )
    return dot(ah, bh) + dot(al, bh) + dot(ah, bl)


def outer(left_ref, right_ref, out_ref, factor, ready):
    for start, stop, first, last in groups(left_ref.shape[0]):
        lhs = jnp.maximum(left_ref[first * HEAD : (last + 1) * HEAD], 0.0)
        product = dot3(split(lhs), split(right_ref[start:stop]), NT)
        for at in range(start, stop, LANE):
            size = min(LANE, stop - at)
            columns = product[:, at - start : at - start + size]
            lane = lax.broadcasted_iota(jnp.int32, (HEAD, size), 1) + at
            total = None
            for head in range(at // HEAD, (at + size - 1) // HEAD + 1):
                block = columns[(head - first) * HEAD : (head - first + 1) * HEAD]
                total = block if total is None else jnp.where(lane >= head * HEAD, block, total)
            total = total * factor
            if size < LANE:
                total = jnp.concatenate(
                    [total, jnp.zeros((HEAD, LANE - size), jnp.float32)], axis=1
                )
            out_ref[at // LANE, 0:HEAD, :] = total
            ready(at // LANE)


def stacked(state):
    high, low = split(state)
    return jnp.concatenate([high, low], axis=0)


def product(weights, x):
    high, low = split(x)
    dot = functools.partial(
        lax.dot_general, dimension_numbers=NN, preferred_element_type=jnp.float32
    )
    both = dot(weights, high)
    return both[:HEAD] + both[HEAD:] + dot(weights[:HEAD], low)


def apply(head, scale, state, field, grads):
    low = head * HEAD // LANE
    high = ((head + 1) * HEAD - 1) // LANE
    offset = head * HEAD - low * LANE
    rows = slice(head * HEAD, (head + 1) * HEAD)

    def pick(at):
        wide = jnp.concatenate([state[at, t, 0:HEAD, :] for t in range(low, high + 1)], axis=1)
        return wide[:, offset : offset + HEAD]

    keys = field[2, rows]
    grad = pick(1)
    query_grad = product(stacked(pick(0) * scale), field[1, rows])
    grads[0, rows] = jnp.where(field[0, rows] > 0, query_grad, 0.0)
    grads[1, rows] = jnp.where(keys > 0, product(stacked(grad), field[3, rows]), 0.0)
    grads[2, rows] = product(stacked(grad.T), jnp.maximum(keys, 0.0))


def exchange(
    frames, chips, spatial_total,
    q_hbm, k_hbm, v_hbm, c_hbm, qg_hbm, kg_hbm, vg_hbm,
    field, grads,
    part_a, part_b, recv_a, chip, recv_b, own, recv_c, recv_e, send_e, state,
    load_sem, a_sem, b_send, b_recv, c_sem, e_sem, x_send, x_recv, m_sem, f_send, f_recv, out_sem,
):
    f, s = lax.axis_index("frame"), lax.axis_index("space")
    x, c = s // CORES, s % CORES
    tiles = part_a.shape[0]
    piece = own.shape[1]
    inner_rows = part_a.shape[1]
    twin = (f, s + 1 - CORES * c)
    mate = (f + 1 - PAIR * (f % PAIR), s)
    step = jnp.where(c == 0, PAIR, -PAIR)
    order = jnp.where(c == 0, f, frames - 1 - f)
    u, odd = order // PAIR, order % PAIR
    last_u = frames // PAIR - 1
    has_before, has_after = u > 0, u < last_u
    before = (jnp.where(has_before, f - step, f), s)
    after = (jnp.where(has_after, f + step, f), s)

    def chip_at(d):
        return (f, (x + d) % chips * CORES + c)

    def remote(src, dst, sems, recv, device):
        return pltpu.make_async_remote_copy(
            src_ref=src, dst_ref=dst, send_sem=sems, recv_sem=recv,
            device_id=device, device_id_type=MESH,
        )

    barrier = pltpu.get_barrier_semaphore()
    partners = [twin, mate] + [chip_at(d) for d in range(1, chips)]
    for device in partners:
        pl.semaphore_signal(barrier, inc=1, device_id=device, device_id_type=MESH)

    @pl.when(has_before)
    def _():
        pl.semaphore_signal(barrier, inc=1, device_id=before, device_id_type=MESH)

    @pl.when(has_after)
    def _():
        pl.semaphore_signal(barrier, inc=1, device_id=after, device_id_type=MESH)

    sources = (q_hbm, c_hbm, k_hbm, v_hbm)
    for core, turn in enumerate(((0, 1, 2, 3), (2, 3, 0, 1))):

        @pl.when(c == core)
        def _():
            for at in turn:
                pltpu.make_async_copy(sources[at].at[0], field.at[at], load_sem.at[at]).start()

    def loaded(at):
        pltpu.make_async_copy(q_hbm.at[0], field.at[at], load_sem.at[at]).wait()

    counts = jnp.full((1, LANE), (f + 1) * (spatial_total * HEAD), jnp.int32)
    scale = (1.0 / jnp.sqrt(counts.astype(jnp.float32)))[0:1, 0:1]

    if inner_rows > HEAD:
        part_a[:, HEAD:, :] = jnp.zeros((tiles, inner_rows - HEAD, LANE), jnp.float32)
        part_b[:, HEAD:, :] = jnp.zeros((tiles, inner_rows - HEAD, LANE), jnp.float32)
    loaded(2 * c)
    loaded(2 * c + 1)
    def copy_a(t):
        return remote(part_a.at[t], recv_a.at[t], a_sem.at[0, t], a_sem.at[1, t], twin)

    def copy_b(d, t):
        rows = pl.ds(pl.multiple_of((x + d) % chips * piece, 8), piece)
        return remote(
            chip.at[t, rows], recv_b.at[d - 1, t],
            b_send.at[d - 1, t], b_recv.at[d - 1, t], chip_at(d),
        )

    def copy_c(t):
        return remote(own.at[t], recv_c.at[t], c_sem.at[0, t], c_sem.at[1, t], mate)

    def copy_e(t):
        return remote(send_e.at[t], recv_e.at[t], e_sem.at[0, t], e_sem.at[1, t], after)

    mine = pl.ds(pl.multiple_of(x * piece, 8), piece)

    def rows_at(d):
        return pl.ds(pl.multiple_of((x + chips - d) % chips * piece, 8), piece)

    def copy_x(d, t):
        here = state.at[c, t, mine]
        return remote(here, here, x_send.at[d - 1, t], x_recv.at[d - 1, t], chip_at(d))

    def copy_m(t):
        here = state.at[c, t, mine]
        return remote(here, here, m_sem.at[0, t], m_sem.at[1, t], twin)

    def copy_f(d, t):
        here = state.at[c, t, rows_at(d)]
        return remote(here, here, f_send.at[d - 1, t], f_recv.at[d - 1, t], twin)

    def send_first(t):
        if t == 0:
            pl.semaphore_wait(
                barrier, len(partners) + has_before.astype(jnp.int32) + has_after.astype(jnp.int32)
            )
        copy_a(t).start()

    outer(field.at[2 * c], field.at[2 * c + 1], part_a, jnp.where(c == 0, scale, 1.0), send_first)
    loaded(2 - 2 * c)
    loaded(3 - 2 * c)
    outer(field.at[2 - 2 * c], field.at[3 - 2 * c], part_b, jnp.where(c == 1, scale, 1.0), lambda t: None)

    def phase_b(t):
        copy_a(t).wait_recv()
        chip[t] = part_b[t] + recv_a[t]
        for d in range(1, chips):
            copy_b(d, t).start()

    def phase_c(t):
        total = chip[t, mine]
        for d in range(1, chips):
            copy_b(d, t).wait_recv()
            total = total + recv_b[d - 1, t]
        own[t] = total
        copy_c(t).start()

    def share(t, entering):
        keep = jnp.where(odd == 1, recv_c[t], 0.0) + own[t]
        state[c, t, mine] = keep if entering is None else keep + entering
        for d in range(1, chips):
            copy_x(d, t).start()
        copy_m(t).start()

    def phase_d(t):
        copy_c(t).wait_recv()

        @pl.when(jnp.logical_not(has_before))
        def _():
            if last_u > 0:
                send_e[t] = own[t] + recv_c[t]
                copy_e(t).start()
            share(t, None)

    def phase_e(t, rank, last):
        @pl.when(u >= rank if last else u == rank)
        def _():
            copy_e(t).wait_recv()

            @pl.when(has_after)
            def _():
                send_e[t] = recv_e[t] + own[t] + recv_c[t]
                copy_e(t).start()

            share(t, recv_e[t])

    def phase_f(t):
        for d in range(1, chips):
            copy_x(d, t).wait_recv()
            copy_f(d, t).start()

    def out_copy(at, head):
        rows = slice(head * HEAD, (head + 1) * HEAD)
        out = (qg_hbm, kg_hbm, vg_hbm)[at]
        return pltpu.make_async_copy(grads.at[at, rows], out.at[0, rows], out_sem.at[at, head])

    def phase_g(t):
        copy_m(t).wait_recv()
        for d in range(1, chips):
            copy_f(d, t).wait_recv()
        for head in range(heads):
            if ((head + 1) * HEAD - 1) // LANE == t:
                apply(head, scale, state, field, grads)
                for at in range(3):
                    out_copy(at, head).start()

    heads = field.shape[1] // HEAD
    events = []
    for t in range(tiles):
        events.append((0.1 * t, 0, functools.partial(phase_b, t)))
        events.append((2.0 + 0.62 * t, 1, functools.partial(phase_c, t)))
        events.append((4.2 + 0.62 * t, 2, functools.partial(phase_d, t)))
        ranks = min(last_u, 3)
        for rank in range(1, ranks + 1):
            events.append((
                4.2 + 2.0 * rank + 0.62 * t, 2 + rank,
                functools.partial(phase_e, t, rank, rank == ranks),
            ))
        events.append((13.0 + 0.62 * t, 9, functools.partial(phase_f, t)))
        events.append((15.0 + 0.62 * t, 10, functools.partial(phase_g, t)))
    for _, _, run in sorted(events, key=lambda e: e[:2]):
        run()

    for t in range(tiles):
        copy_a(t).wait_send()
        copy_c(t).wait_send()
        copy_m(t).wait_send()
        for d in range(1, chips):
            copy_b(d, t).wait_send()
            copy_x(d, t).wait_send()
            copy_f(d, t).wait_send()

    if last_u > 0:

        @pl.when(has_after)
        def _():
            for t in range(tiles):
                copy_e(t).wait_send()

    for head in range(heads):
        for at in range(3):
            out_copy(at, head).wait()


def shards(frames, chips, queries, keys, values, cotangent):
    queries, keys, values, cotangent = (
        jnp.swapaxes(a, 1, 2) for a in (queries, keys, values, cotangent)
    )
    queries, keys, values, cotangent = (
        pltpu.with_memory_space_constraint(a, pltpu.HBM) for a in (queries, keys, values, cotangent)
    )
    _, width, spatial = queries.shape
    spatial_total = spatial * chips * CORES
    tiles = -(-width // LANE)
    piece = -(-HEAD // (8 * chips)) * 8
    rows = piece * chips
    full = pltpu.VMEM((tiles, rows, LANE), jnp.float32)
    part = pltpu.VMEM((tiles, piece, LANE), jnp.float32)
    heads = width // HEAD
    dma = pltpu.SemaphoreType.DMA
    others = max(chips - 1, 1)
    anywhere = pl.BlockSpec(memory_space=pl.ANY)
    shape = jax.ShapeDtypeStruct(queries.shape, jnp.float32)
    grads = pl.pallas_call(
        functools.partial(exchange, frames, chips, spatial_total),
        out_shape=(shape,) * 3,
        in_specs=[pl.BlockSpec(memory_space=pltpu.HBM)] * 4,
        out_specs=(anywhere,) * 3,
        scratch_shapes=[pltpu.VMEM((4, width, spatial), jnp.float32), pltpu.VMEM((3, width, spatial), jnp.float32)]
        + [full, full, full, full, pltpu.VMEM((others, tiles, piece, LANE), jnp.float32)]
        + [part, part, part, part, pltpu.VMEM((2, tiles, rows, LANE), jnp.float32)]
        + [dma((4,)), dma((2, tiles)), dma((others, tiles)), dma((others, tiles))]
        + [dma((2, tiles)), dma((2, tiles)), dma((others, tiles)), dma((others, tiles))]
        + [dma((2, tiles)), dma((others, tiles)), dma((others, tiles)), dma((3, heads))],
        compiler_params=pltpu.CompilerParams(collective_id=0, has_side_effects=True, vmem_limit_bytes=VMEM_LIMIT),
        name="exchange",
    )(queries, keys, values, cotangent)
    return tuple(jnp.swapaxes(a, 1, 2) for a in grads)


def solution(mesh):
    placed = P("frame", "space", None)
    frames, space = mesh.shape["frame"], mesh.shape["space"]
    return jax.shard_map(
        functools.partial(shards, frames, space // CORES),
        mesh=mesh,
        in_specs=(placed,) * 4,
        out_specs=(placed,) * 3,
        check_vma=False,
    )
```

```python
import functools

import jax
import jax.numpy as jnp
from jax import lax
from jax.experimental import pallas as pl
from jax.experimental.pallas import tpu as pltpu
from jax.sharding import PartitionSpec as P

HEAD = 112
LANE = 128
GROUP = 256
CORES = 2
PAIR = 2
VMEM_LIMIT = 32 * 2**20
MESH = pl.DeviceIdType.MESH
NT = (((1,), (1,)), ((), ()))
NN = (((1,), (0,)), ((), ()))


def groups(width):
    found = []
    for start in range(0, width, GROUP):
        stop = min(start + GROUP, width)
        found.append((start, stop, start // HEAD, (stop - 1) // HEAD))
    return found


def split(x):
    high = x.astype(jnp.bfloat16)
    return high, (x - high.astype(jnp.float32)).astype(jnp.bfloat16)


def dot3(a, b, dims):
    (ah, al), (bh, bl) = a, b
    dot = functools.partial(
        lax.dot_general, dimension_numbers=dims, preferred_element_type=jnp.float32
    )
    return dot(ah, bh) + dot(al, bh) + dot(ah, bl)


def outer(left_ref, right_ref, out_ref, factor, ready):
    for start, stop, first, last in groups(left_ref.shape[0]):
        lhs = jnp.maximum(left_ref[first * HEAD : (last + 1) * HEAD], 0.0)
        product = dot3(split(lhs), split(right_ref[start:stop]), NT)
        for at in range(start, stop, LANE):
            size = min(LANE, stop - at)
            columns = product[:, at - start : at - start + size]
            lane = lax.broadcasted_iota(jnp.int32, (HEAD, size), 1) + at
            total = None
            for head in range(at // HEAD, (at + size - 1) // HEAD + 1):
                block = columns[(head - first) * HEAD : (head - first + 1) * HEAD]
                total = block if total is None else jnp.where(lane >= head * HEAD, block, total)
            total = total * factor
            if size < LANE:
                total = jnp.concatenate(
                    [total, jnp.zeros((HEAD, LANE - size), jnp.float32)], axis=1
                )
            out_ref[at // LANE, 0:HEAD, :] = total
            ready(at // LANE)


def stacked(state):
    high, low = split(state)
    return jnp.concatenate([high, low], axis=0)


def product(weights, x):
    high, low = split(x)
    dot = functools.partial(
        lax.dot_general, dimension_numbers=NN, preferred_element_type=jnp.float32
    )
    both = dot(weights, high)
    return both[:HEAD] + both[HEAD:] + dot(weights[:HEAD], low)


def apply(head, scale, state, field, grads):
    low = head * HEAD // LANE
    high = ((head + 1) * HEAD - 1) // LANE
    offset = head * HEAD - low * LANE
    rows = slice(head * HEAD, (head + 1) * HEAD)

    def pick(at):
        wide = jnp.concatenate([state[at, t, 0:HEAD, :] for t in range(low, high + 1)], axis=1)
        return wide[:, offset : offset + HEAD]

    keys = field[2, rows]
    grad = pick(1)
    query_grad = product(stacked(pick(0) * scale), field[1, rows])
    grads[0, rows] = jnp.where(field[0, rows] > 0, query_grad, 0.0)
    grads[1, rows] = jnp.where(keys > 0, product(stacked(grad), field[3, rows]), 0.0)
    grads[2, rows] = product(stacked(grad.T), jnp.maximum(keys, 0.0))


def exchange(
    frames, chips, spatial_total,
    q_hbm, k_hbm, v_hbm, c_hbm, qg_hbm, kg_hbm, vg_hbm,
    field, grads,
    part_a, part_b, recv_a, chip, recv_b, own, recv_c, recv_e, send_e, state,
    load_sem, send_sem, b_send, x_send, f_send,
    a_recv, b_recv, c_recv, e_recv, x_recv, m_recv, f_recv, out_sem,
):
    f, s = lax.axis_index("frame"), lax.axis_index("space")
    x, c = s // CORES, s % CORES
    tiles = part_a.shape[0]
    piece = own.shape[1]
    inner_rows = part_a.shape[1]
    twin = (f, s + 1 - CORES * c)
    mate = (f + 1 - PAIR * (f % PAIR), s)
    step = jnp.where(c == 0, PAIR, -PAIR)
    order = jnp.where(c == 0, f, frames - 1 - f)
    u, odd = order // PAIR, order % PAIR
    last_u = frames // PAIR - 1
    has_before, has_after = u > 0, u < last_u
    before = (jnp.where(has_before, f - step, f), s)
    after = (jnp.where(has_after, f + step, f), s)

    def chip_at(d):
        return (f, (x + d) % chips * CORES + c)

    def remote(src, dst, sems, recv, device):
        return pltpu.make_async_remote_copy(
            src_ref=src, dst_ref=dst, send_sem=sems, recv_sem=recv,
            device_id=device, device_id_type=MESH,
        )

    barrier = pltpu.get_barrier_semaphore()
    partners = [twin, mate] + [chip_at(d) for d in range(1, chips)]
    for device in partners:
        pl.semaphore_signal(barrier, inc=1, device_id=device, device_id_type=MESH)

    @pl.when(has_before)
    def _():
        pl.semaphore_signal(barrier, inc=1, device_id=before, device_id_type=MESH)

    @pl.when(has_after)
    def _():
        pl.semaphore_signal(barrier, inc=1, device_id=after, device_id_type=MESH)

    sources = (q_hbm, c_hbm, k_hbm, v_hbm)
    for core, turn in enumerate(((0, 1, 2, 3), (2, 3, 0, 1))):

        @pl.when(c == core)
        def _():
            for at in turn:
                pltpu.make_async_copy(sources[at].at[0], field.at[at], load_sem.at[at]).start()

    def loaded(at):
        pltpu.make_async_copy(q_hbm.at[0], field.at[at], load_sem.at[at]).wait()

    counts = jnp.full((1, LANE), (f + 1) * (spatial_total * HEAD), jnp.int32)
    scale = (1.0 / jnp.sqrt(counts.astype(jnp.float32)))[0:1, 0:1]

    if inner_rows > HEAD:
        part_a[:, HEAD:, :] = jnp.zeros((tiles, inner_rows - HEAD, LANE), jnp.float32)
        part_b[:, HEAD:, :] = jnp.zeros((tiles, inner_rows - HEAD, LANE), jnp.float32)
    loaded(2 * c)
    loaded(2 * c + 1)
    def copy_a(t):
        return remote(part_a.at[t], recv_a.at[t], send_sem.at[0], a_recv.at[t], twin)

    def copy_b(d, t):
        rows = pl.ds(pl.multiple_of((x + d) % chips * piece, 8), piece)
        return remote(
            chip.at[t, rows], recv_b.at[d - 1, t],
            b_send.at[d - 1], b_recv.at[d - 1, t], chip_at(d),
        )

    def copy_c(t):
        return remote(own.at[t], recv_c.at[t], send_sem.at[1], c_recv.at[t], mate)

    def copy_e(t):
        return remote(send_e.at[t], recv_e.at[t], send_sem.at[2], e_recv.at[t], after)

    mine = pl.ds(pl.multiple_of(x * piece, 8), piece)

    def rows_at(d):
        return pl.ds(pl.multiple_of((x + chips - d) % chips * piece, 8), piece)

    def copy_x(d, t):
        here = state.at[c, t, mine]
        return remote(here, here, x_send.at[d - 1], x_recv.at[d - 1, t], chip_at(d))

    def copy_m(t):
        here = state.at[c, t, mine]
        return remote(here, here, send_sem.at[3], m_recv.at[t], twin)

    def copy_f(d, t):
        here = state.at[c, t, rows_at(d)]
        return remote(here, here, f_send.at[d - 1], f_recv.at[d - 1, t], twin)

    def send_first(t):
        if t == 0:
            pl.semaphore_wait(
                barrier, len(partners) + has_before.astype(jnp.int32) + has_after.astype(jnp.int32)
            )
        copy_a(t).start()

    outer(field.at[2 * c], field.at[2 * c + 1], part_a, jnp.where(c == 0, scale, 1.0), send_first)
    loaded(2 - 2 * c)
    loaded(3 - 2 * c)
    outer(field.at[2 - 2 * c], field.at[3 - 2 * c], part_b, jnp.where(c == 1, scale, 1.0), lambda t: None)

    def phase_b(t):
        copy_a(t).wait_recv()
        chip[t] = part_b[t] + recv_a[t]
        for d in range(1, chips):
            copy_b(d, t).start()

    def phase_c(t):
        total = chip[t, mine]
        for d in range(1, chips):
            copy_b(d, t).wait_recv()
            total = total + recv_b[d - 1, t]
        own[t] = total
        copy_c(t).start()

    def share(t, entering):
        keep = jnp.where(odd == 1, recv_c[t], 0.0) + own[t]
        state[c, t, mine] = keep if entering is None else keep + entering
        for d in range(1, chips):
            copy_x(d, t).start()
        copy_m(t).start()

    def phase_d(t):
        copy_c(t).wait_recv()

        @pl.when(jnp.logical_not(has_before))
        def _():
            if last_u > 0:
                send_e[t] = own[t] + recv_c[t]
                copy_e(t).start()
            share(t, None)

    def phase_e(t, rank, last):
        @pl.when(u >= rank if last else u == rank)
        def _():
            copy_e(t).wait_recv()

            @pl.when(has_after)
            def _():
                send_e[t] = recv_e[t] + own[t] + recv_c[t]
                copy_e(t).start()

            share(t, recv_e[t])

    def phase_f(t):
        for d in range(1, chips):
            copy_x(d, t).wait_recv()
            copy_f(d, t).start()

    def out_copy(at, head):
        rows = slice(head * HEAD, (head + 1) * HEAD)
        out = (qg_hbm, kg_hbm, vg_hbm)[at]
        return pltpu.make_async_copy(grads.at[at, rows], out.at[0, rows], out_sem.at[at])

    def phase_g(t):
        copy_m(t).wait_recv()
        for d in range(1, chips):
            copy_f(d, t).wait_recv()
        for head in range(heads):
            if ((head + 1) * HEAD - 1) // LANE == t:
                apply(head, scale, state, field, grads)
                for at in range(3):
                    out_copy(at, head).start()

    heads = field.shape[1] // HEAD
    events = []
    for t in range(tiles):
        events.append((0.1 * t, 0, functools.partial(phase_b, t)))
        events.append((2.0 + 0.62 * t, 1, functools.partial(phase_c, t)))
        events.append((4.2 + 0.62 * t, 2, functools.partial(phase_d, t)))
        ranks = min(last_u, 3)
        for rank in range(1, ranks + 1):
            events.append((
                4.2 + 2.0 * rank + 0.62 * t, 2 + rank,
                functools.partial(phase_e, t, rank, rank == ranks),
            ))
        events.append((13.0 + 0.62 * t, 9, functools.partial(phase_f, t)))
        events.append((15.0 + 0.62 * t, 10, functools.partial(phase_g, t)))
    for _, _, run in sorted(events, key=lambda e: e[:2]):
        run()

    def sent(buffer, sem):
        remote(buffer, buffer, sem, a_recv.at[0], twin).wait_send()

    sent(part_a, send_sem.at[0])
    sent(own, send_sem.at[1])
    sent(own, send_sem.at[3])
    for d in range(1, chips):
        sent(own, b_send.at[d - 1])
        sent(own, x_send.at[d - 1])
        sent(own, f_send.at[d - 1])

    if last_u > 0:

        @pl.when(has_after)
        def _():
            sent(send_e, send_sem.at[2])

    for at, out in enumerate((qg_hbm, kg_hbm, vg_hbm)):
        pltpu.make_async_copy(grads.at[at], out.at[0], out_sem.at[at]).wait()


def shards(frames, chips, queries, keys, values, cotangent):
    queries, keys, values, cotangent = (
        jnp.swapaxes(a, 1, 2) for a in (queries, keys, values, cotangent)
    )
    queries, keys, values, cotangent = (
        pltpu.with_memory_space_constraint(a, pltpu.HBM) for a in (queries, keys, values, cotangent)
    )
    _, width, spatial = queries.shape
    spatial_total = spatial * chips * CORES
    tiles = -(-width // LANE)
    piece = -(-HEAD // (8 * chips)) * 8
    rows = piece * chips
    full = pltpu.VMEM((tiles, rows, LANE), jnp.float32)
    part = pltpu.VMEM((tiles, piece, LANE), jnp.float32)
    heads = width // HEAD
    dma = pltpu.SemaphoreType.DMA
    others = max(chips - 1, 1)
    anywhere = pl.BlockSpec(memory_space=pl.ANY)
    shape = jax.ShapeDtypeStruct(queries.shape, jnp.float32)
    grads = pl.pallas_call(
        functools.partial(exchange, frames, chips, spatial_total),
        out_shape=(shape,) * 3,
        in_specs=[pl.BlockSpec(memory_space=pltpu.HBM)] * 4,
        out_specs=(anywhere,) * 3,
        scratch_shapes=[pltpu.VMEM((4, width, spatial), jnp.float32), pltpu.VMEM((3, width, spatial), jnp.float32)]
        + [full, full, full, full, pltpu.VMEM((others, tiles, piece, LANE), jnp.float32)]
        + [part, part, part, part, pltpu.VMEM((2, tiles, rows, LANE), jnp.float32)]
        + [dma((4,)), dma((4,)), dma((others,)), dma((others,)), dma((others,))]
        + [dma((tiles,)), dma((others, tiles)), dma((tiles,)), dma((tiles,))]
        + [dma((others, tiles)), dma((tiles,)), dma((others, tiles)), dma((3,))],
        compiler_params=pltpu.CompilerParams(collective_id=0, has_side_effects=True, vmem_limit_bytes=VMEM_LIMIT),
        name="exchange",
    )(queries, keys, values, cotangent)
    return tuple(jnp.swapaxes(a, 1, 2) for a in grads)


def solution(mesh):
    placed = P("frame", "space", None)
    frames, space = mesh.shape["frame"], mesh.shape["space"]
    return jax.shard_map(
        functools.partial(shards, frames, space // CORES),
        mesh=mesh,
        in_specs=(placed,) * 4,
        out_specs=(placed,) * 3,
        check_vma=False,
    )
```
